128 devices in a mesh: leaf: 8 (over x, core), blk: 16 (over z, y).
Axes of the slice: x: 4, y: 4, z: 4, core: 2. Of those that a mesh axis runs over, the one named last changes fastest.
Arguments:
- right_side: float32 [4, 8, 16, 512], P(None, 'leaf', 'blk'), may hold values from -6 to 6
- diag_inverse: bfloat16 [8, 16, 128, 30720], P('leaf', 'blk'), as said below
- update_factor: bfloat16 [8, 16, 128, 69632], P('leaf', 'blk'), may hold values from -0.046875 to 0.046875
- live_blocks: int32 [15], replicated, may hold values from 1 to 128, as said below
Outputs:
- forward_solution: float32 [4, 8, 16, 512], P(None, 'leaf', 'blk')
- solution: float32 [4, 8, 16, 512], P(None, 'leaf', 'blk')
The draws below stay inside these ranges and needn't reach their ends.
Inputs may be any that keep to these rules, and one draw needn't show every extreme that they name: `live_blocks`: A supernode with 2^l * 16 block-rows (level l, listed level by level from level 0, by group within a level) has between a quarter of them (at least 1) and all of them live; the root supernode (the last entry) has all of them live. `diag_inverse`: each level's inverse diagonal block is lower triangular in its supernode's row order, with a positive diagonal.
All inputs are finite; a program needn't handle non-finite values.
Results may differ from the reference program's by a relative error of at most 0.009.
Values sent between devices are 32-bit elements; how exact they have to be, the bound alone decides.
A program may use at most 128 MiB of HBM per device.

```python
import math
import jax
import jax.numpy as jnp
import numpy as np
from jax import lax

BS = 128
NRHS = 4
LEVELS = 4
ROWS = 16384
UCOLS = 69632
N_LEAF = 8
N_BLK = 16


def draw_diag_inverse(key, part):
    level_width = N_BLK * BS
    leaf_position = jnp.arange(N_LEAF).reshape(N_LEAF, 1, 1, 1)
    block_position = jnp.arange(N_BLK).reshape(1, N_BLK, 1, 1)
    row_position = jnp.arange(BS).reshape(1, 1, BS, 1)
    pieces = []
    for height in range(LEVELS):
        supernode_order = 2 ** height * level_width
        level_key = jax.random.fold_in(key, 11 + height)
        noise_key, scale_key = jax.random.split(level_key)
        full_shape = (N_LEAF, N_BLK, BS, supernode_order)
        jitter = jax.random.normal(noise_key, full_shape, jnp.float32)
        diagonal = jax.random.uniform(scale_key, (N_LEAF, N_BLK, BS, 1), jnp.float32, 0.6, 1.6)
        position = (leaf_position % 2 ** height * N_BLK + block_position) * BS + row_position
        column = jnp.arange(supernode_order).reshape(1, 1, 1, supernode_order)
        entries = jnp.where(column < position, jitter * (0.9 / math.sqrt(supernode_order)), jnp.where(column == position, diagonal, 0.0))
        pieces.append(entries)
    return jnp.concatenate(pieces, axis=3).astype(jnp.bfloat16)


def draw_live_blocks(key, part):
    lower_ends = []
    upper_ends = []
    for height in range(LEVELS):
        capacity = 2 ** height * N_BLK
        for group_number in range(N_LEAF // 2 ** height):
            lower_ends.append(max(1, capacity // 4))
            upper_ends.append(capacity + 1)
    lower_table = jnp.array(np.array(lower_ends, dtype=np.int32))
    upper_table = jnp.array(np.array(upper_ends, dtype=np.int32))
    drawn = jax.random.randint(key, (len(lower_ends),), lower_table, upper_table, jnp.int32)
    entry_index = jnp.arange(len(lower_ends)).astype(jnp.int32)
    return jnp.where(entry_index == len(lower_ends) - 1, upper_table - 1, drawn).astype(jnp.int32)


def level_of(key, extent, cuts, least, top_value):
    def one(dim, parts):
        steps = jax.random.uniform(jax.random.fold_in(jax.random.fold_in(key, 6), dim), (parts,), jnp.float32, least / len(cuts), top_value / len(cuts))
        return jnp.repeat(jnp.exp(steps), extent[dim] // parts).reshape((-1,) + (1,) * (len(extent) - dim - 1))

    level = one(*cuts[0])
    for cut in cuts[1:]:
        level = level * one(*cut)
    return level


def gaussian(own_key, shape, width, limit, shards=(), kind=jnp.bfloat16):
    values = width * jax.random.normal(own_key, shape, jnp.float32)
    if shards:
        values = values * level_of(own_key, shape, shards, -0.22, 0.18)
    return jnp.clip(values, -limit, limit).astype(kind)


def setup_inputs(seed: int = 0) -> dict:
    key_of = jax.random.split(jax.random.key(seed), 5)
    return {
        "right_side": gaussian(key_of[0], (NRHS, N_LEAF, N_BLK, LEVELS * BS), 1.0, 6.0, ((1, 8), (2, 16)), jnp.float32),
        "diag_inverse": draw_diag_inverse(jax.random.fold_in(key_of[4], 71), 0),
        "update_factor": gaussian(key_of[2], (N_LEAF, N_BLK, BS, UCOLS), ROWS ** -0.5, 0.046875, ((0, 8), (1, 16))),
        "live_blocks": draw_live_blocks(jax.random.fold_in(key_of[4], 71), 0),
    }


def grouped_product(vectors, matrices, contract_rows):
    vector_count = vectors.shape[0]
    groups = matrices.shape[0]
    stacked = vectors.reshape(vector_count, groups, -1).transpose(1, 0, 2)
    if contract_rows:
        dimension_numbers = (((1,), (0,)), ((), ()))
    else:
        dimension_numbers = (((1,), (1,)), ((), ()))

    def single(operands):
        return lax.dot_general(operands[0], operands[1], dimension_numbers, preferred_element_type=jnp.float32)

    result = lax.map(single, (stacked, matrices))
    return result.transpose(1, 0, 2).reshape(vector_count, -1)


def live_mask(live_blocks, height):
    leaf_position = jnp.arange(N_LEAF).astype(jnp.int32)[:, None]
    block_position = jnp.arange(N_BLK).astype(jnp.int32)[None, :]
    offset = 2 * N_LEAF - (2 * N_LEAF) // (2 ** height)
    counts = live_blocks[offset + leaf_position // (2 ** height)]
    alive = ((leaf_position % (2 ** height)) * N_BLK + block_position < counts).astype(jnp.float32)
    return jnp.broadcast_to(alive[:, :, None], (N_LEAF, N_BLK, BS)).reshape(ROWS)


def reference(right_side, diag_inverse, update_factor, live_blocks):
    level_width = N_BLK * BS
    orders = [(2 ** height) * level_width for height in range(LEVELS)]
    spans = [sum(orders[height + 1:]) for height in range(LEVELS)]
    update_start = [sum(spans[:height]) for height in range(LEVELS)]
    source_rows = right_side.reshape(NRHS, N_LEAF, N_BLK, LEVELS, BS)
    masks = [live_mask(live_blocks, height) for height in range(LEVELS)]

    def inverse_block(height):
        supernode_order = orders[height]
        start = (2 ** height - 1) * level_width
        return diag_inverse[:, :, :, start:start + supernode_order].reshape(N_LEAF // 2 ** height, supernode_order, supernode_order)

    def update_block(cursor, ancestor):
        ancestor_order = orders[ancestor]
        return update_factor[:, :, :, cursor:cursor + ancestor_order].reshape(N_LEAF // 2 ** ancestor, ancestor_order, ancestor_order)

    pending = [jnp.zeros((NRHS, ROWS), jnp.float32) for height in range(LEVELS)]
    forward = []
    for height in range(LEVELS):
        source = source_rows[:, :, :, height, :].reshape(NRHS, ROWS)
        reduced = (masks[height] * (source - pending[height])).astype(jnp.bfloat16)
        solved = masks[height] * grouped_product(reduced, inverse_block(height), False)
        forward.append(solved)
        rounded = solved.astype(jnp.bfloat16)
        cursor = update_start[height]
        for ancestor in range(height + 1, LEVELS):
            pending[ancestor] = pending[ancestor] + grouped_product(rounded, update_block(cursor, ancestor), True)
            cursor += orders[ancestor]

    gathered = [None] * LEVELS
    backward = [None] * LEVELS
    for height in reversed(range(LEVELS)):
        residual = forward[height]
        cursor = update_start[height]
        for ancestor in range(height + 1, LEVELS):
            residual = residual - grouped_product(gathered[ancestor], update_block(cursor, ancestor), False)
            cursor += orders[ancestor]
        weighted = (masks[height] * residual).astype(jnp.bfloat16)
        solved = masks[height] * grouped_product(weighted, inverse_block(height), True)
        backward[height] = solved
        gathered[height] = solved.astype(jnp.bfloat16)

    def arrange(levels_list):
        stacked = jnp.stack([item.reshape(NRHS, N_LEAF, N_BLK, BS) for item in levels_list], axis=3)
        return stacked.reshape(NRHS, N_LEAF, N_BLK, LEVELS * BS)

    return arrange(forward), arrange(backward)
```

```python
import functools

import jax
import jax.numpy as jnp
from jax import lax
from jax.experimental import pallas as pl
from jax.experimental.pallas import tpu as pltpu
from jax.sharding import PartitionSpec as P

MESH = pl.DeviceIdType.MESH
WIDE = 4096
CONTRACT_LAST = (((1,), (1,)), ((), ()))


def split_columns(start, count):
    width = min(WIDE, count)
    return [(start + step, width) for step in range(0, count, width)]


def solve(
    leaf_count,
    block_count,
    block_rows,
    live_ref,
    side_ref,
    inverse_hbm,
    update_hbm,
    forward_ref,
    backward_ref,
    inverse,
    update,
    gathered,
    pending,
    pending_in,
    reduced,
    partials,
    partials_in,
    solved,
    load_sem,
    send_sem,
    recv_sem,
):
    levels = leaf_count.bit_length()
    leaf = lax.axis_index("leaf")
    blk = lax.axis_index("blk")
    level_width = block_count * block_rows
    orders = [(1 << height) * level_width for height in range(levels)]
    sizes = [(1 << height) * block_count for height in range(levels)]
    bases = [(leaf >> height) << height for height in range(levels)]
    ranks = [(leaf - bases[height]) * block_count + blk for height in range(levels)]
    inverse_start = [((1 << height) - 1) * level_width for height in range(levels)]
    update_start = {}
    cursor = 0
    for height in range(levels):
        for ancestor in range(height + 1, levels):
            update_start[ancestor, height] = cursor
            cursor += orders[ancestor]

    loads = {}

    def load(key, hbm, vmem, start, count):
        copy = pltpu.make_async_copy(
            hbm.at[0, 0, :, pl.ds(start, count)],
            vmem.at[:, pl.ds(start, count)],
            load_sem.at[len(loads)],
        )
        copy.start()
        loads[key] = copy

    for height in range(levels):
        load(height, inverse_hbm, inverse, inverse_start[height], orders[height])
        for ancestor in range(height + 1, levels):
            key = (ancestor, height)
            load(key, update_hbm, update, update_start[key], orders[ancestor])

    barrier = pltpu.get_barrier_semaphore()
    for step in range(1, block_count):
        peer = lax.rem(blk + step, block_count)
        pl.semaphore_signal(barrier, inc=1, device_id=(leaf, peer), device_id_type=MESH)
    for step in range(1, leaf_count):
        peer = lax.rem(leaf + step, leaf_count)
        pl.semaphore_signal(barrier, inc=1, device_id=(peer, blk), device_id_type=MESH)
    pl.semaphore_wait(barrier, block_count + leaf_count - 2)

    phases = []

    def exchange(height, source, target, spread):
        size = sizes[height]
        rank = ranks[height]
        base = bases[height]
        phase = len(phases)

        def send(step, carry):
            peer = lax.rem(rank + step, size)
            pltpu.make_async_remote_copy(
                src_ref=source.at[peer] if spread else source.at[rank],
                dst_ref=target.at[rank],
                send_sem=send_sem.at[phase],
                recv_sem=recv_sem.at[phase],
                device_id=(base + peer // block_count, lax.rem(peer, block_count)),
                device_id_type=MESH,
            ).start()
            return carry

        lax.fori_loop(1, size, send, 0)
        bulk = pltpu.make_async_remote_copy(
            src_ref=target.at[pl.ds(0, size - 1)],
            dst_ref=target.at[pl.ds(0, size - 1)],
            send_sem=send_sem.at[phase],
            recv_sem=recv_sem.at[phase],
            device_id=(leaf, blk),
            device_id_type=MESH,
        )
        phases.append(bulk)
        return bulk

    def spread_rows(rows, matrix, start, count, target, add):
        for first, width in split_columns(start, count):
            product = jnp.dot(
                rows, matrix[:, first : first + width], preferred_element_type=jnp.float32
            )
            block = (first - start) // block_rows
            for step in range(width // block_rows):
                piece = product[:, step * block_rows : (step + 1) * block_rows]
                if add:
                    piece = piece + target[block + step]
                target[block + step] = piece

    def gather_rows(vector, matrix, start, count):
        total = None
        for first, width in split_columns(start, count):
            block = (first - start) // block_rows
            pieces = [vector[block + step] for step in range(width // block_rows)]
            piece = lax.dot_general(
                jnp.concatenate(pieces, axis=1).astype(jnp.bfloat16),
                matrix[:, first : first + width],
                CONTRACT_LAST,
                preferred_element_type=jnp.float32,
            )
            total = piece if total is None else total + piece
        return total

    def summed(blocks, count):
        total = blocks[0:8]
        for step in range(8, count, 8):
            total = total + blocks[step : step + 8]
        return jnp.sum(total, axis=0)

    masks = []
    for height in range(levels):
        live_count = live_ref[2 * leaf_count - (2 * leaf_count >> height) + (leaf >> height)]
        masks.append(jnp.where(ranks[height] < live_count, 1.0, 0.0).astype(jnp.float32))
    columns = [slice(height * block_rows, (height + 1) * block_rows) for height in range(levels)]

    forward = []
    for height in range(levels):
        side = side_ref[:, 0, 0, columns[height]]
        rank = ranks[height]
        if height == 0:
            vector = gathered
            vector[rank] = masks[0] * side
        else:
            incoming = pending_in[height - 1]
            vector = reduced[height - 1]
            arrival.wait_recv()
            incoming[rank] = pending[height - 1][rank]
            vector[rank] = masks[height] * (side - summed(incoming, sizes[height]))
        arrival = exchange(height, vector, vector, False)
        loads[height].wait()
        arrival.wait_recv()
        solved_rows = masks[height] * gather_rows(
            vector, inverse, inverse_start[height], orders[height]
        )
        forward.append(solved_rows)
        forward_ref[:, 0, 0, columns[height]] = solved_rows
        rows = solved_rows.astype(jnp.bfloat16)
        for ancestor in range(height + 1, levels):
            key = (ancestor, height)
            loads[key].wait()
            spread_rows(
                rows, update, update_start[key], orders[ancestor], pending[ancestor - 1], height > 0
            )
            if ancestor == height + 1:
                arrival = exchange(ancestor, pending[height], pending_in[height], True)

    residual = list(forward)
    for height in reversed(range(levels)):
        rank = ranks[height]
        rows = (masks[height] * residual[height]).astype(jnp.bfloat16)
        spread_rows(
            rows, inverse, inverse_start[height], orders[height], partials[height], False
        )
        arrival = exchange(height, partials[height], partials_in[height], True)
        if height < levels - 1:
            for lower in range(height):
                key = (height + 1, lower)
                residual[lower] = residual[lower] - gather_rows(
                    solved[height], update, update_start[key], orders[height + 1]
                )
        arrival.wait_recv()
        incoming = partials_in[height]
        incoming[rank] = partials[height][rank]
        whole = masks[height] * summed(incoming, sizes[height])
        backward_ref[:, 0, 0, columns[height]] = whole
        if height > 0:
            vector = solved[height - 1]
            vector[rank] = whole
            arrival = exchange(height, vector, vector, False)
            arrival.wait_recv()
            key = (height, height - 1)
            residual[height - 1] = residual[height - 1] - gather_rows(
                vector, update, update_start[key], orders[height]
            )

    for bulk in phases:
        bulk.wait_send()


def local(leaf_count, block_count, right_side, diag_inverse, update_factor, live_blocks):
    levels = leaf_count.bit_length()
    vectors, _, _, width = right_side.shape
    block_rows = diag_inverse.shape[2]
    sizes = [(1 << height) * block_count for height in range(levels)]

    def blocks(count):
        return pltpu.VMEM((count, vectors, block_rows), jnp.float32)

    upper = [blocks(size) for size in sizes[1:]]
    every = [blocks(size) for size in sizes]
    phases = 4 * levels - 2
    out = jax.ShapeDtypeStruct(right_side.shape, jnp.float32)
    return pl.pallas_call(
        functools.partial(solve, leaf_count, block_count, block_rows),
        out_shape=(out, out),
        in_specs=[
            pl.BlockSpec(memory_space=pltpu.SMEM),
            pl.BlockSpec(memory_space=pltpu.VMEM),
            pl.BlockSpec(memory_space=pl.ANY),
            pl.BlockSpec(memory_space=pl.ANY),
        ],
        out_specs=(
            pl.BlockSpec(memory_space=pltpu.VMEM),
            pl.BlockSpec(memory_space=pltpu.VMEM),
        ),
        scratch_shapes=[
            pltpu.VMEM(diag_inverse.shape[2:], jnp.bfloat16),
            pltpu.VMEM(update_factor.shape[2:], jnp.bfloat16),
            blocks(sizes[0]),
            upper,
            upper,
            upper,
            every,
            every,
            upper,
            pltpu.SemaphoreType.DMA((levels * (levels + 1) // 2,)),
            pltpu.SemaphoreType.DMA((phases,)),
            pltpu.SemaphoreType.DMA((phases,)),
        ],
        compiler_params=pltpu.CompilerParams(
            collective_id=0, has_side_effects=True, vmem_limit_bytes=58 << 20
        ),
        name="solve",
    )(live_blocks, right_side, diag_inverse, update_factor)


def solution(mesh):
    return jax.shard_map(
        functools.partial(local, mesh.shape["leaf"], mesh.shape["blk"]),
        mesh=mesh,
        in_specs=(
            P(None, "leaf", "blk", None),
            P("leaf", "blk", None, None),
            P("leaf", "blk", None, None),
            P(),
        ),
        out_specs=(P(None, "leaf", "blk", None), P(None, "leaf", "blk", None)),
        check_vma=False,
    )
```

```python
import functools
import math

import jax
import jax.numpy as jnp
from jax import lax
from jax.experimental import pallas as pl
from jax.experimental.pallas import tpu as pltpu
from jax.sharding import PartitionSpec as P

MESH = pl.DeviceIdType.MESH
CONTRACT_LAST = (((1,), (1,)), ((), ()))


def far_first(count):
    return sorted(range(count), key=lambda step: -min(step, count - step))


def solve(
    leaf_count,
    block_count,
    block_rows,
    live_ref,
    side_ref,
    inverse_hbm,
    update_hbm,
    forward_ref,
    backward_ref,
    inverse,
    update,
    gathered,
    pending,
    pending_in,
    reduced,
    partials,
    partials_in,
    solved,
    load_sem,
    send_sem,
    recv_sem,
):
    levels = leaf_count.bit_length()
    leaf = lax.axis_index("leaf")
    blk = lax.axis_index("blk")
    level_width = block_count * block_rows
    orders = [(1 << height) * level_width for height in range(levels)]
    sizes = [(1 << height) * block_count for height in range(levels)]
    bases = [(leaf >> height) << height for height in range(levels)]
    ranks = [(leaf - bases[height]) * block_count + blk for height in range(levels)]
    inverse_start = [((1 << height) - 1) * level_width for height in range(levels)]
    update_start = {}
    cursor = 0
    for height in range(levels):
        for ancestor in range(height + 1, levels):
            update_start[ancestor, height] = cursor
            cursor += orders[ancestor]

    loads = {}

    def load(key, hbm, vmem, start, count):
        copy = pltpu.make_async_copy(
            hbm.at[0, 0, :, pl.ds(start, count)],
            vmem.at[:, pl.ds(start, count)],
            load_sem.at[len(loads)],
        )
        copy.start()
        loads[key] = copy

    for height in range(levels):
        load(height, inverse_hbm, inverse, inverse_start[height], orders[height])
        for ancestor in range(height + 1, levels):
            key = (ancestor, height)
            load(key, update_hbm, update, update_start[key], orders[ancestor])

    barrier = pltpu.get_barrier_semaphore()
    for step in range(1, block_count):
        peer = lax.rem(blk + step, block_count)
        pl.semaphore_signal(barrier, inc=1, device_id=(leaf, peer), device_id_type=MESH)
    for step in range(1, leaf_count):
        peer = lax.rem(leaf + step, leaf_count)
        pl.semaphore_signal(barrier, inc=1, device_id=(peer, blk), device_id_type=MESH)
    pl.semaphore_wait(barrier, block_count + leaf_count - 2)

    side = math.isqrt(block_count)
    row, column = blk // side, lax.rem(blk, side)
    core = lax.rem(leaf, 2)
    chips = [max(1, (1 << height) // 2) for height in range(levels)]
    cores = [min(2, 1 << height) for height in range(levels)]
    chunks = [cores[height] * block_count for height in range(levels)]
    own_chip = [(leaf - bases[height]) // 2 for height in range(levels)]
    phases = []

    def chip_at(height, step):
        return lax.rem(own_chip[height] + step, chips[height])

    def exchange(height, source, target, spread, make=None):
        phase = len(phases)
        rank = ranks[height]
        phases.append((height, target))
        for step in far_first(chips[height]):
            chip = chip_at(height, step)
            if make is not None:
                make(chip)

            def send(index, carry, step=step, chip=chip):
                away = lax.rem(side + side // 2 - index, side)
                to_row = lax.rem(row + away, side)
                for across in far_first(side):
                    to_blk = to_row * side + lax.rem(column + across, side)
                    for other in reversed(range(cores[height])):
                        if height == 0:
                            to_leaf = leaf
                        else:
                            to_leaf = bases[height] + 2 * chip + lax.rem(core + other, 2)
                        peer = (to_leaf - bases[height]) * block_count + to_blk
                        copy = pltpu.make_async_remote_copy(
                            src_ref=source.at[peer] if spread else source.at[rank],
                            dst_ref=target.at[rank],
                            send_sem=send_sem.at[phase],
                            recv_sem=recv_sem.at[phase, (chips[height] - step) % chips[height]],
                            device_id=(to_leaf, to_blk),
                            device_id_type=MESH,
                        )
                        if step == 0 and across == 0 and other == 0:
                            pl.when(away != 0)(copy.start)
                        else:
                            copy.start()
                return carry

            lax.fori_loop(0, side, send, 0)
        return phase

    def bulk(phase, count, step):
        target = phases[phase][1]
        return pltpu.make_async_remote_copy(
            src_ref=target.at[pl.ds(0, count)],
            dst_ref=target.at[pl.ds(0, count)],
            send_sem=send_sem.at[phase],
            recv_sem=recv_sem.at[phase, step],
            device_id=(leaf, blk),
            device_id_type=MESH,
        )

    def arrivals(phase):
        height = phases[phase][0]
        for step in reversed(far_first(chips[height])):
            bulk(phase, chunks[height] - (step == 0), step).wait_recv()
            yield chip_at(height, step)

    def spread_rows(height, rows, matrix, start, chip, target, add):
        count = chunks[height]
        width = count * block_rows
        first = pl.multiple_of(start + chip * width, width // cores[height])
        product = jnp.dot(
            rows, matrix[:, pl.ds(first, width)], preferred_element_type=jnp.float32
        )
        for step in range(count):
            piece = product[:, step * block_rows : (step + 1) * block_rows]
            if add:
                piece = piece + target[chip * count + step]
            target[chip * count + step] = piece

    def gather_rows(height, vector, matrix, start, chip):
        count = chunks[height]
        width = count * block_rows
        first = pl.multiple_of(start + chip * width, width // cores[height])
        pieces = [vector[chip * count + step] for step in range(count)]
        return lax.dot_general(
            jnp.concatenate(pieces, axis=1).astype(jnp.bfloat16),
            matrix[:, pl.ds(first, width)],
            CONTRACT_LAST,
            preferred_element_type=jnp.float32,
        )

    def summed(phase, source):
        height, target = phases[phase]
        target[ranks[height]] = source[ranks[height]]
        count = chunks[height]
        total = None
        for chip in arrivals(phase):
            for step in range(0, count, 8):
                piece = target[pl.ds(chip * count + step, 8)]
                total = piece if total is None else total + piece
        return jnp.sum(total, axis=0)

    masks = []
    for height in range(levels):
        live_count = live_ref[2 * leaf_count - (2 * leaf_count >> height) + (leaf >> height)]
        masks.append(jnp.where(ranks[height] < live_count, 1.0, 0.0).astype(jnp.float32))
    columns = [slice(height * block_rows, (height + 1) * block_rows) for height in range(levels)]

    forward = []
    arriving = None
    for height in range(levels):
        side_rows = side_ref[:, 0, 0, columns[height]]
        rank = ranks[height]
        if height == 0:
            vector = gathered
        else:
            vector = reduced[height - 1]
            side_rows = side_rows - summed(arriving, pending[height - 1])
        vector[rank] = masks[height] * side_rows
        phase = exchange(height, vector, vector, False)
        loads[height].wait()
        product = jnp.zeros_like(side_rows)
        for chip in arrivals(phase):
            product = product + gather_rows(
                height, vector, inverse, inverse_start[height], chip
            )
        solved_rows = masks[height] * product
        forward.append(solved_rows)
        forward_ref[:, 0, 0, columns[height]] = solved_rows
        rows = solved_rows.astype(jnp.bfloat16)
        for ancestor in range(height + 1, levels):
            key = (ancestor, height)
            loads[key].wait()

            def make(chip, ancestor=ancestor, rows=rows, key=key, add=height > 0):
                target = pending[ancestor - 1]
                spread_rows(ancestor, rows, update, update_start[key], chip, target, add)

            if ancestor == height + 1:
                arriving = exchange(
                    ancestor, pending[height], pending_in[height], True, make
                )
            else:
                for chip in range(chips[ancestor]):
                    make(chip)

    residual = list(forward)
    for height in reversed(range(levels)):
        rank = ranks[height]
        rows = (masks[height] * residual[height]).astype(jnp.bfloat16)

        def make(chip, height=height, rows=rows):
            start = inverse_start[height]
            spread_rows(height, rows, inverse, start, chip, partials[height], False)

        arriving = exchange(height, partials[height], partials_in[height], True, make)
        if height < levels - 1:
            for lower in range(height):
                for chip in range(chips[height + 1]):
                    residual[lower] = residual[lower] - gather_rows(
                        height + 1,
                        solved[height],
                        update,
                        update_start[height + 1, lower],
                        chip,
                    )
        whole = masks[height] * summed(arriving, partials[height])
        backward_ref[:, 0, 0, columns[height]] = whole
        if height > 0:
            vector = solved[height - 1]
            vector[rank] = whole
            phase = exchange(height, vector, vector, False)
            for chip in arrivals(phase):
                residual[height - 1] = residual[height - 1] - gather_rows(
                    height, vector, update, update_start[height, height - 1], chip
                )

    for phase, (height, _) in enumerate(phases):
        bulk(phase, sizes[height] - 1, 0).wait_send()


def local(leaf_count, block_count, right_side, diag_inverse, update_factor, live_blocks):
    levels = leaf_count.bit_length()
    vectors, _, _, width = right_side.shape
    block_rows = diag_inverse.shape[2]
    sizes = [(1 << height) * block_count for height in range(levels)]

    def blocks(count):
        return pltpu.VMEM((count, vectors, block_rows), jnp.float32)

    upper = [blocks(size) for size in sizes[1:]]
    every = [blocks(size) for size in sizes]
    phases = 4 * levels - 2
    out = jax.ShapeDtypeStruct(right_side.shape, jnp.float32)
    return pl.pallas_call(
        functools.partial(solve, leaf_count, block_count, block_rows),
        out_shape=(out, out),
        in_specs=[
            pl.BlockSpec(memory_space=pltpu.SMEM),
            pl.BlockSpec(memory_space=pltpu.VMEM),
            pl.BlockSpec(memory_space=pl.ANY),
            pl.BlockSpec(memory_space=pl.ANY),
        ],
        out_specs=(
            pl.BlockSpec(memory_space=pltpu.VMEM),
            pl.BlockSpec(memory_space=pltpu.VMEM),
        ),
        scratch_shapes=[
            pltpu.VMEM(diag_inverse.shape[2:], jnp.bfloat16),
            pltpu.VMEM(update_factor.shape[2:], jnp.bfloat16),
            blocks(sizes[0]),
            upper,
            upper,
            upper,
            every,
            every,
            upper,
            pltpu.SemaphoreType.DMA((levels * (levels + 1) // 2,)),
            pltpu.SemaphoreType.DMA((phases,)),
            pltpu.SemaphoreType.DMA((phases, max(1, leaf_count // 2))),
        ],
        compiler_params=pltpu.CompilerParams(
            collective_id=0, has_side_effects=True, vmem_limit_bytes=58 << 20
        ),
        name="solve",
    )(live_blocks, right_side, diag_inverse, update_factor)


def solution(mesh):
    return jax.shard_map(
        functools.partial(local, mesh.shape["leaf"], mesh.shape["blk"]),
        mesh=mesh,
        in_specs=(
            P(None, "leaf", "blk", None),
            P("leaf", "blk", None, None),
            P("leaf", "blk", None, None),
            P(),
        ),
        out_specs=(P(None, "leaf", "blk", None), P(None, "leaf", "blk", None)),
        check_vma=False,
    )
```

```python
import functools
import itertools
import math

import jax
import jax.numpy as jnp
from jax import lax
from jax.experimental import pallas as pl
from jax.experimental.pallas import tpu as pltpu
from jax.sharding import PartitionSpec as P

MESH = pl.DeviceIdType.MESH
EARLY = 2
PLACE = pltpu.VMEM
USE_WIDE = False
CONTRACT_LAST = (((1,), (1,)), ((), ()))


def ring(step, count):
    return min(step, count - step)


def solve(
    leaf_count,
    block_count,
    block_rows,
    live_ref,
    side_ref,
    inverse_hbm,
    update_hbm,
    forward_ref,
    backward_ref,
    inverse,
    update,
    gathered,
    pending,
    pending_in,
    reduced,
    partials,
    partials_in,
    solved,
    load_sem,
    send_sem,
    recv_sem,
):
    levels = leaf_count.bit_length()
    leaf = lax.axis_index("leaf")
    blk = lax.axis_index("blk")
    level_width = block_count * block_rows
    orders = [(1 << height) * level_width for height in range(levels)]
    sizes = [(1 << height) * block_count for height in range(levels)]
    bases = [(leaf >> height) << height for height in range(levels)]
    ranks = [(leaf - bases[height]) * block_count + blk for height in range(levels)]
    inverse_start = [((1 << height) - 1) * level_width for height in range(levels)]
    update_start = {}
    cursor = 0
    for height in range(levels):
        for ancestor in range(height + 1, levels):
            update_start[ancestor, height] = cursor
            cursor += orders[ancestor]

    loads = {}

    def load(key, hbm, vmem, start, count):
        copy = pltpu.make_async_copy(
            hbm.at[0, 0, :, pl.ds(start, count)],
            vmem.at[:, pl.ds(start, count)],
            load_sem.at[len(loads)],
        )
        copy.start()
        loads[key] = copy

    for height in range(levels):
        load(height, inverse_hbm, inverse, inverse_start[height], orders[height])
        for ancestor in range(height + 1, levels):
            key = (ancestor, height)
            load(key, update_hbm, update, update_start[key], orders[ancestor])

    barrier = pltpu.get_barrier_semaphore()
    for step in range(1, block_count):
        peer = lax.rem(blk + step, block_count)
        pl.semaphore_signal(barrier, inc=1, device_id=(leaf, peer), device_id_type=MESH)
    for step in range(1, leaf_count):
        peer = lax.rem(leaf + step, leaf_count)
        pl.semaphore_signal(barrier, inc=1, device_id=(peer, blk), device_id_type=MESH)
    pl.semaphore_wait(barrier, block_count + leaf_count - 2)

    side = math.isqrt(block_count)
    core = lax.rem(leaf, 2)
    chips = [max(1, (1 << height) // 2) for height in range(levels)]
    cores = [min(2, 1 << height) for height in range(levels)]
    to_row = [lax.rem(blk // side + step, side) for step in range(side)]
    to_column = [lax.rem(blk + step, side) for step in range(side)]
    to_blk = {
        (down, across): to_row[down] * side + to_column[across]
        for down in range(side)
        for across in range(side)
    }
    to_leaf = {(0, 0, 0): 0}
    for height in range(1, levels):
        own_chip = (leaf - bases[height]) // 2
        for step in range(chips[height]):
            chip = lax.rem(own_chip + step, chips[height])
            for other in range(2):
                to_leaf[height, step, other] = 2 * chip + lax.rem(core + other, 2)
    phases = []

    def hops(height, step, down, across):
        return ring(step, chips[height]) + ring(down, side) + ring(across, side)

    def exchange(height, source, target, make=None):
        phase = len(phases)
        rank = ranks[height]
        phases.append((height, target))
        paths = sorted(
            itertools.product(
                range(chips[height]), range(side), range(side), reversed(range(cores[height]))
            ),
            key=lambda path: -hops(height, *path[:3]),
        )
        longest = hops(height, *paths[0][:3])

        def send(step, down, across, other):
            if step == down == across == other == 0:
                return
            place = to_leaf[height, step, other]
            peer = place * block_count + to_blk[down, across]
            arrival = (chips[height] - step) % chips[height] * 2 + other
            pltpu.make_async_remote_copy(
                src_ref=source.at[rank if make is None else peer],
                dst_ref=target.at[rank],
                send_sem=send_sem.at[phase],
                recv_sem=recv_sem.at[phase, arrival],
                device_id=(bases[height] + place, to_blk[down, across]),
                device_id_type=MESH,
            ).start()

        held = []
        for step in sorted(range(chips[height]), key=lambda step: -ring(step, chips[height])):
            if make is not None:
                make(step)
            for path in paths:
                if path[0] != step:
                    continue
                if make is not None and hops(height, *path[:3]) >= longest - EARLY:
                    send(*path)
                else:
                    held.append(path)
        for path in sorted(held, key=paths.index):
            send(*path)
        return phase

    def bulk(phase, count, arrival):
        target = phases[phase][1]
        return pltpu.make_async_remote_copy(
            src_ref=target.at[pl.ds(0, count)],
            dst_ref=target.at[pl.ds(0, count)],
            send_sem=send_sem.at[phase],
            recv_sem=recv_sem.at[phase, arrival],
            device_id=(leaf, blk),
            device_id_type=MESH,
        )

    def arrivals(phase):
        height = phases[phase][0]
        for step in sorted(range(chips[height]), key=lambda step: ring(step, chips[height])):
            leaves = []
            for other in range(cores[height]):
                count = block_count - (step == other == 0)
                bulk(phase, count, step * 2 + other).wait_recv()
                leaves.append(to_leaf[height, step, other])
                if not USE_WIDE:
                    yield leaves[0], 1
                    leaves = []
            if leaves:
                yield leaves[0] // 2 * 2 if height > 0 else 0, len(leaves)

    def spread_rows(rows, matrix, start, first, count, target, add):
        column = pl.multiple_of(start + first * level_width, level_width)
        product = jnp.dot(
            rows, matrix[:, pl.ds(column, count * level_width)], preferred_element_type=jnp.float32
        )
        for step in range(count * block_count):
            piece = product[:, step * block_rows : (step + 1) * block_rows]
            if add:
                piece = piece + target[first * block_count + step]
            target[first * block_count + step] = piece

    def gather_rows(vector, matrix, start, first, count):
        column = pl.multiple_of(start + first * level_width, level_width)
        pieces = [vector[first * block_count + step] for step in range(count * block_count)]
        return lax.dot_general(
            jnp.concatenate(pieces, axis=1).astype(jnp.bfloat16),
            matrix[:, pl.ds(column, count * level_width)],
            CONTRACT_LAST,
            preferred_element_type=jnp.float32,
        )

    def summed(phase, source):
        height, target = phases[phase]
        target[ranks[height]] = source[ranks[height]]
        total = None
        for first, count in arrivals(phase):
            for step in range(0, count * block_count, 8):
                piece = target[pl.ds(first * block_count + step, 8)]
                total = piece if total is None else total + piece
        return jnp.sum(total, axis=0)

    masks = []
    for height in range(levels):
        live_count = live_ref[2 * leaf_count - (2 * leaf_count >> height) + (leaf >> height)]
        masks.append(jnp.where(ranks[height] < live_count, 1.0, 0.0).astype(jnp.float32))
    columns = [slice(height * block_rows, (height + 1) * block_rows) for height in range(levels)]

    forward = []
    arriving = None
    for height in range(levels):
        side_rows = side_ref[:, 0, 0, columns[height]]
        rank = ranks[height]
        if height == 0:
            vector = gathered
        else:
            vector = reduced[height - 1]
            side_rows = side_rows - summed(arriving, pending[height - 1])
        vector[rank] = masks[height] * side_rows
        phase = exchange(height, vector, vector)
        loads[height].wait()
        product = jnp.zeros_like(side_rows)
        for first, count in arrivals(phase):
            product = product + gather_rows(
                    vector, inverse, inverse_start[height], first, count
                )
        solved_rows = masks[height] * product
        forward.append(solved_rows)
        forward_ref[:, 0, 0, columns[height]] = solved_rows
        rows = solved_rows.astype(jnp.bfloat16)
        for ancestor in range(height + 1, levels):
            key = (ancestor, height)
            loads[key].wait()

            def spread(first, ancestor=ancestor, rows=rows, key=key, add=height > 0):
                target = pending[ancestor - 1]
                spread_rows(rows, update, update_start[key], first, 2, target, add)

            if ancestor == height + 1:

                def make(step, ancestor=ancestor, spread=spread):
                    spread(to_leaf[ancestor, step, 0] // 2 * 2)

                arriving = exchange(ancestor, pending[height], pending_in[height], make)
            else:
                for first in range(0, 1 << ancestor, 2):
                    spread(first)

    residual = list(forward)
    for height in reversed(range(levels)):
        rank = ranks[height]
        rows = (masks[height] * residual[height]).astype(jnp.bfloat16)

        def make(step, height=height, rows=rows):
            first = to_leaf[height, step, 0] // 2 * 2
            spread_rows(
                rows,
                inverse,
                inverse_start[height],
                first,
                cores[height],
                partials[height],
                False,
            )

        arriving = exchange(height, partials[height], partials_in[height], make)
        if height < levels - 1:
            for lower in range(height):
                start = update_start[height + 1, lower]
                for first in range(0, 2 << height, 2):
                    residual[lower] = residual[lower] - gather_rows(
                        solved[height], update, start, first, 2
                    )
        whole = masks[height] * summed(arriving, partials[height])
        backward_ref[:, 0, 0, columns[height]] = whole
        if height > 0:
            vector = solved[height - 1]
            vector[rank] = whole
            phase = exchange(height, vector, vector)
            for first, count in arrivals(phase):
                residual[height - 1] = residual[height - 1] - gather_rows(
                    vector, update, update_start[height, height - 1], first, count
                )

    for phase, (height, _) in enumerate(phases):
        bulk(phase, sizes[height] - 1, 0).wait_send()


def place(forward_ref, backward_ref, forward_out, backward_out, sem):
    first = pltpu.make_async_copy(forward_ref, forward_out, sem.at[0])
    second = pltpu.make_async_copy(backward_ref, backward_out, sem.at[1])
    first.start()
    second.start()
    first.wait()
    second.wait()


def local(leaf_count, block_count, right_side, diag_inverse, update_factor, live_blocks):
    levels = leaf_count.bit_length()
    vectors, _, _, width = right_side.shape
    block_rows = diag_inverse.shape[2]
    sizes = [(1 << height) * block_count for height in range(levels)]

    def blocks(count):
        return pltpu.VMEM((count, vectors, block_rows), jnp.float32)

    upper = [blocks(size) for size in sizes[1:]]
    every = [blocks(size) for size in sizes]
    phases = 4 * levels - 2
    out = jax.ShapeDtypeStruct(right_side.shape, jnp.float32)
    solutions = pl.pallas_call(
        functools.partial(solve, leaf_count, block_count, block_rows),
        out_shape=(out, out),
        in_specs=[
            pl.BlockSpec(memory_space=pltpu.SMEM),
            pl.BlockSpec(memory_space=pltpu.VMEM),
            pl.BlockSpec(memory_space=pl.ANY),
            pl.BlockSpec(memory_space=pl.ANY),
        ],
        out_specs=(
            pl.BlockSpec(memory_space=pltpu.VMEM),
            pl.BlockSpec(memory_space=pltpu.VMEM),
        ),
        scratch_shapes=[
            pltpu.VMEM(diag_inverse.shape[2:], jnp.bfloat16),
            pltpu.VMEM(update_factor.shape[2:], jnp.bfloat16),
            blocks(sizes[0]),
            upper,
            upper,
            upper,
            every,
            every,
            upper,
            pltpu.SemaphoreType.DMA((levels * (levels + 1) // 2,)),
            pltpu.SemaphoreType.DMA((phases,)),
            pltpu.SemaphoreType.DMA((phases, leaf_count)),
        ],
        compiler_params=pltpu.CompilerParams(
            collective_id=0, has_side_effects=True, vmem_limit_bytes=58 << 20
        ),
        name="solve",
    )(live_blocks, right_side, diag_inverse, update_factor)
    return pl.pallas_call(
        place,
        out_shape=(out, out),
        in_specs=[pl.BlockSpec(memory_space=PLACE)] * 2,
        out_specs=(pl.BlockSpec(memory_space=pl.ANY),) * 2,
        scratch_shapes=[pltpu.SemaphoreType.DMA((2,))],
        name="place",
    )(*solutions)


def solution(mesh):
    return jax.shard_map(
        functools.partial(local, mesh.shape["leaf"], mesh.shape["blk"]),
        mesh=mesh,
        in_specs=(
            P(None, "leaf", "blk", None),
            P("leaf", "blk", None, None),
            P("leaf", "blk", None, None),
            P(),
        ),
        out_specs=(P(None, "leaf", "blk", None), P(None, "leaf", "blk", None)),
        check_vma=False,
    )
```

```python
import functools
import itertools
import math

import jax
import jax.numpy as jnp
from jax import lax
from jax.experimental import pallas as pl
from jax.experimental.pallas import tpu as pltpu
from jax.sharding import PartitionSpec as P

MESH = pl.DeviceIdType.MESH
EARLY = 2
PLACE = pltpu.VMEM
USE_WIDE = False
CONTRACT_LAST = (((1,), (1,)), ((), ()))


def ring(step, count):
    return min(step, count - step)


def solve(
    leaf_count,
    block_count,
    block_rows,
    live_ref,
    side_ref,
    inverse_hbm,
    update_hbm,
    forward_ref,
    backward_ref,
    inverse,
    update,
    gathered,
    pending,
    pending_in,
    reduced,
    partials,
    partials_in,
    solved,
    one_row,
    eight_rows,
    load_sem,
    send_sem,
    recv_sem,
):
    levels = leaf_count.bit_length()
    leaf = lax.axis_index("leaf")
    blk = lax.axis_index("blk")
    level_width = block_count * block_rows
    orders = [(1 << height) * level_width for height in range(levels)]
    sizes = [(1 << height) * block_count for height in range(levels)]
    bases = [(leaf >> height) << height for height in range(levels)]
    ranks = [(leaf - bases[height]) * block_count + blk for height in range(levels)]
    inverse_start = [((1 << height) - 1) * level_width for height in range(levels)]
    update_start = {}
    cursor = 0
    for height in range(levels):
        for ancestor in range(height + 1, levels):
            update_start[ancestor, height] = cursor
            cursor += orders[ancestor]

    loads = {}

    def load(key, hbm, vmem, start, count):
        copy = pltpu.make_async_copy(
            hbm.at[0, 0, :, pl.ds(start, count)],
            vmem.at[:, pl.ds(start, count)],
            load_sem.at[len(loads)],
        )
        copy.start()
        loads[key] = copy

    for height in range(levels):
        load(height, inverse_hbm, inverse, inverse_start[height], orders[height])
        for ancestor in range(height + 1, levels):
            key = (ancestor, height)
            load(key, update_hbm, update, update_start[key], orders[ancestor])

    barrier = pltpu.get_barrier_semaphore()
    for step in range(1, block_count):
        peer = lax.rem(blk + step, block_count)
        pl.semaphore_signal(barrier, inc=1, device_id=(leaf, peer), device_id_type=MESH)
    for step in range(1, leaf_count):
        peer = lax.rem(leaf + step, leaf_count)
        pl.semaphore_signal(barrier, inc=1, device_id=(peer, blk), device_id_type=MESH)
    pl.semaphore_wait(barrier, block_count + leaf_count - 2)

    side = math.isqrt(block_count)
    core = lax.rem(leaf, 2)
    chips = [max(1, (1 << height) // 2) for height in range(levels)]
    cores = [min(2, 1 << height) for height in range(levels)]
    to_row = [lax.rem(blk // side + step, side) for step in range(side)]
    to_column = [lax.rem(blk + step, side) for step in range(side)]
    to_blk = {
        (down, across): to_row[down] * side + to_column[across]
        for down in range(side)
        for across in range(side)
    }
    to_leaf = {(0, 0, 0): 0}
    for height in range(1, levels):
        own_chip = (leaf - bases[height]) // 2
        for step in range(chips[height]):
            chip = lax.rem(own_chip + step, chips[height])
            for other in range(2):
                to_leaf[height, step, other] = 2 * chip + lax.rem(core + other, 2)
    own_chips = [(leaf - bases[height]) // 2 for height in range(levels)]
    phases = []

    def guarded(condition, body):
        if condition is None:
            body()
        else:
            pl.when(condition)(body)

    def meets(height, step, upward):
        if upward is None or step == 0:
            return None
        if upward:
            return own_chips[height] + step < chips[height]
        return own_chips[height] + step >= chips[height]

    def hops(height, step, down, across):
        return ring(step, chips[height]) + ring(down, side) + ring(across, side)

    def exchange(height, source, target, make=None, upward=None):
        phase = len(phases)
        rank = ranks[height]
        phases.append((height, target, upward))
        paths = sorted(
            itertools.product(
                range(chips[height]), range(side), range(side), reversed(range(cores[height]))
            ),
            key=lambda path: -hops(height, *path[:3]),
        )
        longest = hops(height, *paths[0][:3])

        def send(step, down, across, other):
            if step == down == across == other == 0:
                return
            place = to_leaf[height, step, other]
            peer = place * block_count + to_blk[down, across]
            arrival = (chips[height] - step) % chips[height] * 2 + other
            pltpu.make_async_remote_copy(
                src_ref=source.at[rank if make is None else peer],
                dst_ref=target.at[rank],
                send_sem=send_sem.at[phase],
                recv_sem=recv_sem.at[phase, arrival],
                device_id=(bases[height] + place, to_blk[down, across]),
                device_id_type=MESH,
            ).start()

        held = []
        for step in sorted(range(chips[height]), key=lambda step: -ring(step, chips[height])):
            reach = [path for path in paths if path[0] == step]

            def serve(step=step, reach=reach):
                if make is not None:
                    make(step)
                for path in reach:
                    late = hops(height, *path[:3]) < longest - EARLY
                    if upward is None and (make is None or late):
                        held.append(path)
                    else:
                        send(*path)

            guarded(meets(height, step, upward), serve)
        for path in sorted(held, key=paths.index):
            send(*path)
        return phase

    def bulk(phase, count, arrival):
        target = phases[phase][1]
        return pltpu.make_async_remote_copy(
            src_ref=target.at[pl.ds(0, count)],
            dst_ref=target.at[pl.ds(0, count)],
            send_sem=send_sem.at[phase],
            recv_sem=recv_sem.at[phase, arrival],
            device_id=(leaf, blk),
            device_id_type=MESH,
        )

    def receive(phase, use):
        height, _, upward = phases[phase]
        for step in sorted(range(chips[height]), key=lambda step: ring(step, chips[height])):

            def take(step=step):
                for other in range(cores[height]):
                    count = block_count - (step == other == 0)
                    bulk(phase, count, step * 2 + other).wait_recv()
                    if not USE_WIDE:
                        use(to_leaf[height, step, other], 1)
                if USE_WIDE:
                    use(to_leaf[height, step, 0] // 2 * 2 if height > 0 else 0, cores[height])

            guarded(meets(height, step, None if upward is None else not upward), take)

    def collect(phase, term, held):
        if phases[phase][2] is None:
            terms = []
            receive(phase, lambda first, count: terms.append(term(first, count)))
            return functools.reduce(jnp.add, terms)
        fresh = [True]

        def use(first, count):
            if fresh[0]:
                held[...] = term(first, count)
                fresh[0] = False
            else:
                held[...] = held[...] + term(first, count)

        receive(phase, use)
        return held[...]

    def spread_rows(rows, matrix, start, first, count, target, add):
        column = pl.multiple_of(start + first * level_width, level_width)
        product = jnp.dot(
            rows, matrix[:, pl.ds(column, count * level_width)], preferred_element_type=jnp.float32
        )
        for step in range(count * block_count):
            piece = product[:, step * block_rows : (step + 1) * block_rows]
            if add:
                piece = piece + target[first * block_count + step]
            target[first * block_count + step] = piece

    def gather_rows(vector, matrix, start, first, count):
        column = pl.multiple_of(start + first * level_width, level_width)
        pieces = [vector[first * block_count + step] for step in range(count * block_count)]
        return lax.dot_general(
            jnp.concatenate(pieces, axis=1).astype(jnp.bfloat16),
            matrix[:, pl.ds(column, count * level_width)],
            CONTRACT_LAST,
            preferred_element_type=jnp.float32,
        )

    def summed(phase, source):
        height, target, _ = phases[phase]
        target[ranks[height]] = source[ranks[height]]

        def term(first, count):
            total = None
            for step in range(0, count * block_count, 8):
                piece = target[pl.ds(first * block_count + step, 8)]
                total = piece if total is None else total + piece
            return total

        return jnp.sum(collect(phase, term, eight_rows), axis=0)

    masks = []
    for height in range(levels):
        live_count = live_ref[2 * leaf_count - (2 * leaf_count >> height) + (leaf >> height)]
        masks.append(jnp.where(ranks[height] < live_count, 1.0, 0.0).astype(jnp.float32))
    columns = [slice(height * block_rows, (height + 1) * block_rows) for height in range(levels)]

    forward = []
    arriving = None
    for height in range(levels):
        side_rows = side_ref[:, 0, 0, columns[height]]
        rank = ranks[height]
        if height == 0:
            vector = gathered
        else:
            vector = reduced[height - 1]
            side_rows = side_rows - summed(arriving, pending[height - 1])
        vector[rank] = masks[height] * side_rows
        phase = exchange(height, vector, vector, upward=True if chips[height] > 1 else None)
        loads[height].wait()
        start = inverse_start[height]
        product = collect(
            phase,
            lambda first, count: gather_rows(vector, inverse, start, first, count),
            one_row,
        )
        solved_rows = masks[height] * product
        forward.append(solved_rows)
        forward_ref[:, 0, 0, columns[height]] = solved_rows
        rows = solved_rows.astype(jnp.bfloat16)
        for ancestor in range(height + 1, levels):
            key = (ancestor, height)
            loads[key].wait()

            def spread(first, ancestor=ancestor, rows=rows, key=key, add=height > 0):
                target = pending[ancestor - 1]
                spread_rows(rows, update, update_start[key], first, 2, target, add)

            if ancestor == height + 1:

                def make(step, ancestor=ancestor, spread=spread):
                    spread(to_leaf[ancestor, step, 0] // 2 * 2)

                arriving = exchange(ancestor, pending[height], pending_in[height], make)
            else:
                for first in range(0, 1 << ancestor, 2):
                    spread(first)

    residual = list(forward)
    for height in reversed(range(levels)):
        rank = ranks[height]
        rows = (masks[height] * residual[height]).astype(jnp.bfloat16)

        def make(step, height=height, rows=rows):
            first = to_leaf[height, step, 0] // 2 * 2
            spread_rows(
                rows,
                inverse,
                inverse_start[height],
                first,
                cores[height],
                partials[height],
                False,
            )

        upward = False if chips[height] > 1 else None
        arriving = exchange(height, partials[height], partials_in[height], make, upward)
        if height < levels - 1:
            for lower in range(height):
                start = update_start[height + 1, lower]
                for first in range(0, 2 << height, 2):
                    residual[lower] = residual[lower] - gather_rows(
                        solved[height], update, start, first, 2
                    )
        whole = masks[height] * summed(arriving, partials[height])
        backward_ref[:, 0, 0, columns[height]] = whole
        if height > 0:
            vector = solved[height - 1]
            vector[rank] = whole
            phase = exchange(height, vector, vector)
            start = update_start[height, height - 1]
            residual[height - 1] = residual[height - 1] - collect(
                phase,
                lambda first, count: gather_rows(vector, update, start, first, count),
                one_row,
            )

    for phase, (height, _, upward) in enumerate(phases):
        if upward is None:
            bulk(phase, sizes[height] - 1, 0).wait_send()
            continue
        for step in range(chips[height]):
            count = cores[height] * block_count - (step == 0)
            guarded(meets(height, step, upward), bulk(phase, count, 0).wait_send)


def place(forward_ref, backward_ref, forward_out, backward_out, sem):
    first = pltpu.make_async_copy(forward_ref, forward_out, sem.at[0])
    second = pltpu.make_async_copy(backward_ref, backward_out, sem.at[1])
    first.start()
    second.start()
    first.wait()
    second.wait()


def local(leaf_count, block_count, right_side, diag_inverse, update_factor, live_blocks):
    levels = leaf_count.bit_length()
    vectors, _, _, width = right_side.shape
    block_rows = diag_inverse.shape[2]
    sizes = [(1 << height) * block_count for height in range(levels)]

    def blocks(count):
        return pltpu.VMEM((count, vectors, block_rows), jnp.float32)

    upper = [blocks(size) for size in sizes[1:]]
    every = [blocks(size) for size in sizes]
    phases = 4 * levels - 2
    out = jax.ShapeDtypeStruct(right_side.shape, jnp.float32)
    solutions = pl.pallas_call(
        functools.partial(solve, leaf_count, block_count, block_rows),
        out_shape=(out, out),
        in_specs=[
            pl.BlockSpec(memory_space=pltpu.SMEM),
            pl.BlockSpec(memory_space=pltpu.VMEM),
            pl.BlockSpec(memory_space=pl.ANY),
            pl.BlockSpec(memory_space=pl.ANY),
        ],
        out_specs=(
            pl.BlockSpec(memory_space=pltpu.VMEM),
            pl.BlockSpec(memory_space=pltpu.VMEM),
        ),
        scratch_shapes=[
            pltpu.VMEM(diag_inverse.shape[2:], jnp.bfloat16),
            pltpu.VMEM(update_factor.shape[2:], jnp.bfloat16),
            blocks(sizes[0]),
            upper,
            upper,
            upper,
            every,
            every,
            upper,
            pltpu.VMEM((vectors, block_rows), jnp.float32),
            blocks(8),
            pltpu.SemaphoreType.DMA((levels * (levels + 1) // 2,)),
            pltpu.SemaphoreType.DMA((phases,)),
            pltpu.SemaphoreType.DMA((phases, leaf_count)),
        ],
        compiler_params=pltpu.CompilerParams(
            collective_id=0, has_side_effects=True, vmem_limit_bytes=58 << 20
        ),
        name="solve",
    )(live_blocks, right_side, diag_inverse, update_factor)
    return pl.pallas_call(
        place,
        out_shape=(out, out),
        in_specs=[pl.BlockSpec(memory_space=PLACE)] * 2,
        out_specs=(pl.BlockSpec(memory_space=pl.ANY),) * 2,
        scratch_shapes=[pltpu.SemaphoreType.DMA((2,))],
        name="place",
    )(*solutions)


def solution(mesh):
    return jax.shard_map(
        functools.partial(local, mesh.shape["leaf"], mesh.shape["blk"]),
        mesh=mesh,
        in_specs=(
            P(None, "leaf", "blk", None),
            P("leaf", "blk", None, None),
            P("leaf", "blk", None, None),
            P(),
        ),
        out_specs=(P(None, "leaf", "blk", None), P(None, "leaf", "blk", None)),
        check_vma=False,
    )
```

```python
import functools
import itertools
import math

import jax
import jax.numpy as jnp
from jax import lax
from jax.experimental import pallas as pl
from jax.experimental.pallas import tpu as pltpu
from jax.sharding import PartitionSpec as P

MESH = pl.DeviceIdType.MESH
EARLY = 2
CONTRACT_LAST = (((1,), (1,)), ((), ()))


def ring(step, count):
    return min(step, count - step)


def solve(
    leaf_count,
    block_count,
    block_rows,
    live_ref,
    side_ref,
    inverse_hbm,
    update_hbm,
    forward_ref,
    backward_ref,
    inverse,
    update,
    gathered,
    pending,
    pending_in,
    reduced,
    partials,
    partials_in,
    solved,
    one_row,
    eight_rows,
    load_sem,
    send_sem,
    recv_sem,
):
    levels = leaf_count.bit_length()
    leaf = lax.axis_index("leaf")
    blk = lax.axis_index("blk")
    level_width = block_count * block_rows
    orders = [(1 << height) * level_width for height in range(levels)]
    sizes = [(1 << height) * block_count for height in range(levels)]
    bases = [(leaf >> height) << height for height in range(levels)]
    ranks = [(leaf - bases[height]) * block_count + blk for height in range(levels)]
    inverse_start = [((1 << height) - 1) * level_width for height in range(levels)]
    update_start = {}
    cursor = 0
    for height in range(levels):
        for ancestor in range(height + 1, levels):
            update_start[ancestor, height] = cursor
            cursor += orders[ancestor]

    loads = {}

    def load(key, hbm, vmem, start, count):
        copy = pltpu.make_async_copy(
            hbm.at[0, 0, :, pl.ds(start, count)],
            vmem.at[:, pl.ds(start, count)],
            load_sem.at[len(loads)],
        )
        copy.start()
        loads[key] = copy

    for height in range(levels):
        load(height, inverse_hbm, inverse, inverse_start[height], orders[height])
        for ancestor in range(height + 1, levels):
            key = (ancestor, height)
            load(key, update_hbm, update, update_start[key], orders[ancestor])

    barrier = pltpu.get_barrier_semaphore()
    for step in range(1, block_count):
        peer = lax.rem(blk + step, block_count)
        pl.semaphore_signal(barrier, inc=1, device_id=(leaf, peer), device_id_type=MESH)
    for step in range(1, leaf_count):
        peer = lax.rem(leaf + step, leaf_count)
        pl.semaphore_signal(barrier, inc=1, device_id=(peer, blk), device_id_type=MESH)
    pl.semaphore_wait(barrier, block_count + leaf_count - 2)

    side = math.isqrt(block_count)
    core = lax.rem(leaf, 2)
    chips = [max(1, (1 << height) // 2) for height in range(levels)]
    cores = [min(2, 1 << height) for height in range(levels)]
    to_row = [lax.rem(blk // side + step, side) for step in range(side)]
    to_column = [lax.rem(blk + step, side) for step in range(side)]
    to_blk = {
        (down, across): to_row[down] * side + to_column[across]
        for down in range(side)
        for across in range(side)
    }
    to_leaf = {(0, 0, 0): 0}
    for height in range(1, levels):
        own_chip = (leaf - bases[height]) // 2
        for step in range(chips[height]):
            chip = lax.rem(own_chip + step, chips[height])
            for other in range(2):
                to_leaf[height, step, other] = 2 * chip + lax.rem(core + other, 2)
    own_chips = [(leaf - bases[height]) // 2 for height in range(levels)]
    phases = []

    def guarded(condition, body):
        if condition is None:
            body()
        else:
            pl.when(condition)(body)

    def meets(height, step, other, upward):
        if upward is None or step == other == 0:
            return None
        if step == 0:
            return core == (0 if upward else 1)
        if upward:
            return own_chips[height] + step < chips[height]
        return own_chips[height] + step >= chips[height]

    def hops(height, step, down, across):
        return ring(step, chips[height]) + ring(down, side) + ring(across, side)

    def exchange(height, source, target, make=None, upward=None):
        phase = len(phases)
        rank = ranks[height]
        phases.append((height, target, upward))
        paths = sorted(
            itertools.product(
                range(chips[height]), range(side), range(side), reversed(range(cores[height]))
            ),
            key=lambda path: -hops(height, *path[:3]),
        )
        longest = hops(height, *paths[0][:3])

        def send(step, down, across, other):
            if step == down == across == other == 0:
                return
            place = to_leaf[height, step, other]
            peer = place * block_count + to_blk[down, across]
            arrival = (chips[height] - step) % chips[height] * 2 + other
            pltpu.make_async_remote_copy(
                src_ref=source.at[rank if make is None else peer],
                dst_ref=target.at[rank],
                send_sem=send_sem.at[phase],
                recv_sem=recv_sem.at[phase, arrival],
                device_id=(bases[height] + place, to_blk[down, across]),
                device_id_type=MESH,
            ).start()

        held = []
        for step in sorted(range(chips[height]), key=lambda step: -ring(step, chips[height])):
            reach = [path for path in paths if path[0] == step]

            def serve(step=step, reach=reach):
                if make is not None:
                    make(step)
                for path in reach:
                    late = hops(height, *path[:3]) < longest - EARLY
                    if upward is not None and step == 0:
                        continue
                    if upward is None and (make is None or late):
                        held.append(path)
                    else:
                        send(*path)

            guarded(None if step == 0 else meets(height, step, 0, upward), serve)
            if upward is not None and step == 0:
                for other in reversed(range(cores[height])):

                    def share(other=other, reach=reach):
                        for path in reach:
                            if path[3] == other:
                                send(*path)

                    guarded(meets(height, 0, other, upward), share)
        for path in sorted(held, key=paths.index):
            send(*path)
        return phase

    def bulk(phase, count, arrival):
        target = phases[phase][1]
        return pltpu.make_async_remote_copy(
            src_ref=target.at[pl.ds(0, count)],
            dst_ref=target.at[pl.ds(0, count)],
            send_sem=send_sem.at[phase],
            recv_sem=recv_sem.at[phase, arrival],
            device_id=(leaf, blk),
            device_id_type=MESH,
        )

    def receive(phase, use):
        height, _, upward = phases[phase]
        for step in sorted(range(chips[height]), key=lambda step: ring(step, chips[height])):

            for other in range(cores[height]):

                def take(step=step, other=other):
                    count = block_count - (step == other == 0)
                    bulk(phase, count, step * 2 + other).wait_recv()
                    use(to_leaf[height, step, other], 1)

                needed = None if upward is None else not upward
                guarded(meets(height, step, other, needed), take)

    def collect(phase, term, held):
        if phases[phase][2] is None:
            terms = []
            receive(phase, lambda first, count: terms.append(term(first, count)))
            return functools.reduce(jnp.add, terms)
        fresh = [True]

        def use(first, count):
            if fresh[0]:
                held[...] = term(first, count)
                fresh[0] = False
            else:
                held[...] = held[...] + term(first, count)

        receive(phase, use)
        return held[...]

    def spread_rows(rows, matrix, start, first, count, target, add):
        column = pl.multiple_of(start + first * level_width, level_width)
        product = jnp.dot(
            rows, matrix[:, pl.ds(column, count * level_width)], preferred_element_type=jnp.float32
        )
        for step in range(count * block_count):
            piece = product[:, step * block_rows : (step + 1) * block_rows]
            if add:
                piece = piece + target[first * block_count + step]
            target[first * block_count + step] = piece

    def gather_rows(vector, matrix, start, first, count):
        column = pl.multiple_of(start + first * level_width, level_width)
        pieces = [vector[first * block_count + step] for step in range(count * block_count)]
        return lax.dot_general(
            jnp.concatenate(pieces, axis=1).astype(jnp.bfloat16),
            matrix[:, pl.ds(column, count * level_width)],
            CONTRACT_LAST,
            preferred_element_type=jnp.float32,
        )

    def summed(phase, source):
        height, target, _ = phases[phase]
        target[ranks[height]] = source[ranks[height]]

        def term(first, count):
            total = None
            for step in range(0, count * block_count, 8):
                piece = target[pl.ds(first * block_count + step, 8)]
                total = piece if total is None else total + piece
            return total

        return jnp.sum(collect(phase, term, eight_rows), axis=0)

    masks = []
    for height in range(levels):
        live_count = live_ref[2 * leaf_count - (2 * leaf_count >> height) + (leaf >> height)]
        masks.append(jnp.where(ranks[height] < live_count, 1.0, 0.0).astype(jnp.float32))
    columns = [slice(height * block_rows, (height + 1) * block_rows) for height in range(levels)]

    forward = []
    arriving = None
    for height in range(levels):
        side_rows = side_ref[:, 0, 0, columns[height]]
        rank = ranks[height]
        if height == 0:
            vector = gathered
        else:
            vector = reduced[height - 1]
            side_rows = side_rows - summed(arriving, pending[height - 1])
        vector[rank] = masks[height] * side_rows
        phase = exchange(height, vector, vector, upward=True if height > 0 else None)
        loads[height].wait()
        start = inverse_start[height]
        product = collect(
            phase,
            lambda first, count: gather_rows(vector, inverse, start, first, count),
            one_row,
        )
        solved_rows = masks[height] * product
        forward.append(solved_rows)
        forward_ref[:, 0, 0, columns[height]] = solved_rows
        rows = solved_rows.astype(jnp.bfloat16)
        for ancestor in range(height + 1, levels):
            key = (ancestor, height)
            loads[key].wait()

            def spread(first, ancestor=ancestor, rows=rows, key=key, add=height > 0):
                target = pending[ancestor - 1]
                spread_rows(rows, update, update_start[key], first, 2, target, add)

            if ancestor == height + 1:

                def make(step, ancestor=ancestor, spread=spread):
                    spread(to_leaf[ancestor, step, 0] // 2 * 2)

                arriving = exchange(ancestor, pending[height], pending_in[height], make)
            else:
                for first in range(0, 1 << ancestor, 2):
                    spread(first)

    residual = list(forward)
    for height in reversed(range(levels)):
        rank = ranks[height]
        rows = (masks[height] * residual[height]).astype(jnp.bfloat16)

        def make(step, height=height, rows=rows):
            first = to_leaf[height, step, 0] // 2 * 2
            spread_rows(
                rows,
                inverse,
                inverse_start[height],
                first,
                cores[height],
                partials[height],
                False,
            )

        upward = False if height > 0 else None
        arriving = exchange(height, partials[height], partials_in[height], make, upward)
        if height < levels - 1:
            for lower in range(height):
                start = update_start[height + 1, lower]
                for first in range(0, 2 << height, 2):
                    residual[lower] = residual[lower] - gather_rows(
                        solved[height], update, start, first, 2
                    )
        whole = masks[height] * summed(arriving, partials[height])
        backward_ref[:, 0, 0, columns[height]] = whole
        if height > 0:
            vector = solved[height - 1]
            vector[rank] = whole
            phase = exchange(height, vector, vector)
            start = update_start[height, height - 1]
            residual[height - 1] = residual[height - 1] - collect(
                phase,
                lambda first, count: gather_rows(vector, update, start, first, count),
                one_row,
            )

    for phase, (height, _, upward) in enumerate(phases):
        if upward is None:
            bulk(phase, sizes[height] - 1, 0).wait_send()
            continue
        for step, other in itertools.product(range(chips[height]), range(cores[height])):
            count = block_count - (step == other == 0)
            guarded(meets(height, step, other, upward), bulk(phase, count, 0).wait_send)


def place(forward_ref, backward_ref, forward_out, backward_out, sem):
    first = pltpu.make_async_copy(forward_ref, forward_out, sem.at[0])
    second = pltpu.make_async_copy(backward_ref, backward_out, sem.at[1])
    first.start()
    second.start()
    first.wait()
    second.wait()


def local(leaf_count, block_count, right_side, diag_inverse, update_factor, live_blocks):
    levels = leaf_count.bit_length()
    vectors, _, _, width = right_side.shape
    block_rows = diag_inverse.shape[2]
    sizes = [(1 << height) * block_count for height in range(levels)]

    def blocks(count):
        return pltpu.VMEM((count, vectors, block_rows), jnp.float32)

    upper = [blocks(size) for size in sizes[1:]]
    every = [blocks(size) for size in sizes]
    phases = 4 * levels - 2
    out = jax.ShapeDtypeStruct(right_side.shape, jnp.float32)
    kept = pltpu.VMEM(right_side.shape, jnp.float32)
    solutions = pl.pallas_call(
        functools.partial(solve, leaf_count, block_count, block_rows),
        out_shape=(kept, kept),
        in_specs=[
            pl.BlockSpec(memory_space=pltpu.SMEM),
            pl.BlockSpec(memory_space=pltpu.VMEM),
            pl.BlockSpec(memory_space=pl.ANY),
            pl.BlockSpec(memory_space=pl.ANY),
        ],
        out_specs=(
            pl.BlockSpec(memory_space=pltpu.VMEM),
            pl.BlockSpec(memory_space=pltpu.VMEM),
        ),
        scratch_shapes=[
            pltpu.VMEM(diag_inverse.shape[2:], jnp.bfloat16),
            pltpu.VMEM(update_factor.shape[2:], jnp.bfloat16),
            blocks(sizes[0]),
            upper,
            upper,
            upper,
            every,
            every,
            upper,
            pltpu.VMEM((vectors, block_rows), jnp.float32),
            blocks(8),
            pltpu.SemaphoreType.DMA((levels * (levels + 1) // 2,)),
            pltpu.SemaphoreType.DMA((phases,)),
            pltpu.SemaphoreType.DMA((phases, leaf_count)),
        ],
        compiler_params=pltpu.CompilerParams(
            collective_id=0, has_side_effects=True, vmem_limit_bytes=58 << 20
        ),
        name="solve",
    )(live_blocks, right_side, diag_inverse, update_factor)
    return pl.pallas_call(
        place,
        out_shape=(out, out),
        in_specs=[pl.BlockSpec(memory_space=pltpu.VMEM)] * 2,
        compiler_params=pltpu.CompilerParams(vmem_limit_bytes=1 << 20),
        out_specs=(pl.BlockSpec(memory_space=pl.ANY),) * 2,
        scratch_shapes=[pltpu.SemaphoreType.DMA((2,))],
        name="place",
    )(*solutions)


def solution(mesh):
    return jax.shard_map(
        functools.partial(local, mesh.shape["leaf"], mesh.shape["blk"]),
        mesh=mesh,
        in_specs=(
            P(None, "leaf", "blk", None),
            P("leaf", "blk", None, None),
            P("leaf", "blk", None, None),
            P(),
        ),
        out_specs=(P(None, "leaf", "blk", None), P(None, "leaf", "blk", None)),
        check_vma=False,
    )
```

```python
import functools
import itertools
import math

import jax
import jax.numpy as jnp
from jax import lax
from jax.experimental import pallas as pl
from jax.experimental.pallas import tpu as pltpu
from jax.sharding import PartitionSpec as P

MESH = pl.DeviceIdType.MESH
EARLY = 2
CONTRACT_LAST = (((1,), (1,)), ((), ()))


def ring(step, count):
    return min(step, count - step)


def solve(
    leaf_count,
    block_count,
    block_rows,
    live_ref,
    side_ref,
    inverse_hbm,
    update_hbm,
    forward_ref,
    backward_ref,
    inverse,
    update,
    gathered,
    pending,
    pending_in,
    reduced,
    partials,
    partials_in,
    solved,
    one_row,
    eight_rows,
    load_sem,
    send_sem,
    recv_sem,
):
    levels = leaf_count.bit_length()
    leaf = lax.axis_index("leaf")
    blk = lax.axis_index("blk")
    level_width = block_count * block_rows
    orders = [(1 << height) * level_width for height in range(levels)]
    sizes = [(1 << height) * block_count for height in range(levels)]
    bases = [(leaf >> height) << height for height in range(levels)]
    ranks = [(leaf - bases[height]) * block_count + blk for height in range(levels)]
    inverse_start = [((1 << height) - 1) * level_width for height in range(levels)]
    update_start = {}
    cursor = 0
    for height in range(levels):
        for ancestor in range(height + 1, levels):
            update_start[ancestor, height] = cursor
            cursor += orders[ancestor]

    loads = {}

    def load(key, hbm, vmem, start, count):
        copy = pltpu.make_async_copy(
            hbm.at[0, 0, :, pl.ds(start, count)],
            vmem.at[:, pl.ds(start, count)],
            load_sem.at[len(loads)],
        )
        copy.start()
        loads[key] = copy

    for height in range(levels):
        load(height, inverse_hbm, inverse, inverse_start[height], orders[height])
        for ancestor in range(height + 1, levels):
            key = (ancestor, height)
            load(key, update_hbm, update, update_start[key], orders[ancestor])

    barrier = pltpu.get_barrier_semaphore()
    edge = math.isqrt(block_count)
    for down, across in sorted(
        itertools.product(range(edge), range(edge)),
        key=lambda way: -ring(way[0], edge) - ring(way[1], edge),
    ):
        if down == across == 0:
            continue
        peer = lax.rem(blk // edge + down, edge) * edge + lax.rem(blk + across, edge)
        pl.semaphore_signal(barrier, inc=1, device_id=(leaf, peer), device_id_type=MESH)
    for step in sorted(range(1, leaf_count), key=lambda step: -ring(step, leaf_count)):
        peer = lax.rem(leaf + step, leaf_count)
        pl.semaphore_signal(barrier, inc=1, device_id=(peer, blk), device_id_type=MESH)
    pl.semaphore_wait(barrier, block_count + leaf_count - 2)

    side = math.isqrt(block_count)
    core = lax.rem(leaf, 2)
    chips = [max(1, (1 << height) // 2) for height in range(levels)]
    cores = [min(2, 1 << height) for height in range(levels)]
    to_row = [lax.rem(blk // side + step, side) for step in range(side)]
    to_column = [lax.rem(blk + step, side) for step in range(side)]
    to_blk = {
        (down, across): to_row[down] * side + to_column[across]
        for down in range(side)
        for across in range(side)
    }
    to_leaf = {(0, 0, 0): 0}
    for height in range(1, levels):
        own_chip = (leaf - bases[height]) // 2
        for step in range(chips[height]):
            chip = lax.rem(own_chip + step, chips[height])
            for other in range(2):
                to_leaf[height, step, other] = 2 * chip + lax.rem(core + other, 2)
    own_chips = [(leaf - bases[height]) // 2 for height in range(levels)]
    phases = []

    def guarded(condition, body):
        if condition is None:
            body()
        else:
            pl.when(condition)(body)

    def meets(height, step, other, upward):
        if upward is None or step == other == 0:
            return None
        if step == 0:
            return core == (0 if upward else 1)
        if upward:
            return own_chips[height] + step < chips[height]
        return own_chips[height] + step >= chips[height]

    def hops(height, step, down, across):
        return ring(step, chips[height]) + ring(down, side) + ring(across, side)

    def exchange(height, source, target, make=None, upward=None):
        phase = len(phases)
        rank = ranks[height]
        phases.append((height, target, upward))
        paths = sorted(
            itertools.product(
                range(chips[height]), range(side), range(side), reversed(range(cores[height]))
            ),
            key=lambda path: -hops(height, *path[:3]),
        )
        longest = hops(height, *paths[0][:3])

        def send(step, down, across, other):
            if step == down == across == other == 0:
                return
            place = to_leaf[height, step, other]
            peer = place * block_count + to_blk[down, across]
            arrival = (chips[height] - step) % chips[height] * 2 + other
            pltpu.make_async_remote_copy(
                src_ref=source.at[rank if make is None else peer],
                dst_ref=target.at[rank],
                send_sem=send_sem.at[phase],
                recv_sem=recv_sem.at[phase, arrival],
                device_id=(bases[height] + place, to_blk[down, across]),
                device_id_type=MESH,
            ).start()

        held = []
        for step in sorted(range(chips[height]), key=lambda step: -ring(step, chips[height])):
            reach = [path for path in paths if path[0] == step]

            def serve(step=step, reach=reach):
                if make is not None:
                    make(step)
                for path in reach:
                    late = hops(height, *path[:3]) < longest - EARLY
                    if upward is not None and step == 0:
                        continue
                    if upward is None and (make is None or late):
                        held.append(path)
                    else:
                        send(*path)

            guarded(None if step == 0 else meets(height, step, 0, upward), serve)
            if upward is not None and step == 0:
                for other in reversed(range(cores[height])):

                    def share(other=other, reach=reach):
                        for path in reach:
                            if path[3] == other:
                                send(*path)

                    guarded(meets(height, 0, other, upward), share)
        for path in sorted(held, key=paths.index):
            send(*path)
        return phase

    def bulk(phase, count, arrival):
        target = phases[phase][1]
        return pltpu.make_async_remote_copy(
            src_ref=target.at[pl.ds(0, count)],
            dst_ref=target.at[pl.ds(0, count)],
            send_sem=send_sem.at[phase],
            recv_sem=recv_sem.at[phase, arrival],
            device_id=(leaf, blk),
            device_id_type=MESH,
        )

    def receive(phase, use):
        height, _, upward = phases[phase]
        for step in sorted(range(chips[height]), key=lambda step: ring(step, chips[height])):

            for other in range(cores[height]):

                def take(step=step, other=other):
                    count = block_count - (step == other == 0)
                    bulk(phase, count, step * 2 + other).wait_recv()
                    use(to_leaf[height, step, other], 1)

                needed = None if upward is None else not upward
                guarded(meets(height, step, other, needed), take)

    def collect(phase, term, held):
        if phases[phase][2] is None:
            terms = []
            receive(phase, lambda first, count: terms.append(term(first, count)))
            return functools.reduce(jnp.add, terms)
        fresh = [True]

        def use(first, count):
            if fresh[0]:
                held[...] = term(first, count)
                fresh[0] = False
            else:
                held[...] = held[...] + term(first, count)

        receive(phase, use)
        return held[...]

    def spread_rows(rows, matrix, start, first, count, target, add):
        column = pl.multiple_of(start + first * level_width, level_width)
        product = jnp.dot(
            rows, matrix[:, pl.ds(column, count * level_width)], preferred_element_type=jnp.float32
        )
        for step in range(count * block_count):
            piece = product[:, step * block_rows : (step + 1) * block_rows]
            if add:
                piece = piece + target[first * block_count + step]
            target[first * block_count + step] = piece

    def gather_rows(vector, matrix, start, first, count):
        column = pl.multiple_of(start + first * level_width, level_width)
        pieces = [vector[first * block_count + step] for step in range(count * block_count)]
        return lax.dot_general(
            jnp.concatenate(pieces, axis=1).astype(jnp.bfloat16),
            matrix[:, pl.ds(column, count * level_width)],
            CONTRACT_LAST,
            preferred_element_type=jnp.float32,
        )

    def summed(phase, source):
        height, target, _ = phases[phase]
        target[ranks[height]] = source[ranks[height]]

        def term(first, count):
            total = None
            for step in range(0, count * block_count, 8):
                piece = target[pl.ds(first * block_count + step, 8)]
                total = piece if total is None else total + piece
            return total

        return jnp.sum(collect(phase, term, eight_rows), axis=0)

    masks = []
    for height in range(levels):
        live_count = live_ref[2 * leaf_count - (2 * leaf_count >> height) + (leaf >> height)]
        masks.append(jnp.where(ranks[height] < live_count, 1.0, 0.0).astype(jnp.float32))
    columns = [slice(height * block_rows, (height + 1) * block_rows) for height in range(levels)]

    forward = []
    arriving = None
    for height in range(levels):
        side_rows = side_ref[:, 0, 0, columns[height]]
        rank = ranks[height]
        if height == 0:
            vector = gathered
        else:
            vector = reduced[height - 1]
            side_rows = side_rows - summed(arriving, pending[height - 1])
        vector[rank] = masks[height] * side_rows
        phase = exchange(height, vector, vector, upward=True if height > 0 else None)
        loads[height].wait()
        start = inverse_start[height]
        product = collect(
            phase,
            lambda first, count: gather_rows(vector, inverse, start, first, count),
            one_row,
        )
        solved_rows = masks[height] * product
        forward.append(solved_rows)
        forward_ref[:, 0, 0, columns[height]] = solved_rows
        rows = solved_rows.astype(jnp.bfloat16)
        for ancestor in range(height + 1, levels):
            key = (ancestor, height)
            loads[key].wait()

            def spread(first, ancestor=ancestor, rows=rows, key=key, add=height > 0):
                target = pending[ancestor - 1]
                spread_rows(rows, update, update_start[key], first, 2, target, add)

            if ancestor == height + 1:

                def make(step, ancestor=ancestor, spread=spread):
                    spread(to_leaf[ancestor, step, 0] // 2 * 2)

                arriving = exchange(ancestor, pending[height], pending_in[height], make)
            else:
                for first in range(0, 1 << ancestor, 2):
                    spread(first)

    residual = list(forward)
    for height in reversed(range(levels)):
        rank = ranks[height]
        rows = (masks[height] * residual[height]).astype(jnp.bfloat16)

        def make(step, height=height, rows=rows):
            first = to_leaf[height, step, 0] // 2 * 2
            spread_rows(
                rows,
                inverse,
                inverse_start[height],
                first,
                cores[height],
                partials[height],
                False,
            )

        upward = False if height > 0 else None
        arriving = exchange(height, partials[height], partials_in[height], make, upward)
        if height < levels - 1:
            for lower in range(height):
                start = update_start[height + 1, lower]
                for first in range(0, 2 << height, 2):
                    residual[lower] = residual[lower] - gather_rows(
                        solved[height], update, start, first, 2
                    )
        whole = masks[height] * summed(arriving, partials[height])
        backward_ref[:, 0, 0, columns[height]] = whole
        if height > 0:
            vector = solved[height - 1]
            vector[rank] = whole
            phase = exchange(height, vector, vector)
            start = update_start[height, height - 1]
            residual[height - 1] = residual[height - 1] - collect(
                phase,
                lambda first, count: gather_rows(vector, update, start, first, count),
                one_row,
            )

    for phase, (height, _, upward) in enumerate(phases):
        if upward is None:
            bulk(phase, sizes[height] - 1, 0).wait_send()
            continue
        for step, other in itertools.product(range(chips[height]), range(cores[height])):
            count = block_count - (step == other == 0)
            guarded(meets(height, step, other, upward), bulk(phase, count, 0).wait_send)


def place(forward_ref, backward_ref, forward_out, backward_out, sem):
    first = pltpu.make_async_copy(forward_ref, forward_out, sem.at[0])
    second = pltpu.make_async_copy(backward_ref, backward_out, sem.at[1])
    first.start()
    second.start()
    first.wait()
    second.wait()


def local(leaf_count, block_count, right_side, diag_inverse, update_factor, live_blocks):
    levels = leaf_count.bit_length()
    vectors, _, _, width = right_side.shape
    block_rows = diag_inverse.shape[2]
    sizes = [(1 << height) * block_count for height in range(levels)]

    def blocks(count):
        return pltpu.VMEM((count, vectors, block_rows), jnp.float32)

    upper = [blocks(size) for size in sizes[1:]]
    every = [blocks(size) for size in sizes]
    phases = 4 * levels - 2
    out = jax.ShapeDtypeStruct(right_side.shape, jnp.float32)
    kept = pltpu.VMEM(right_side.shape, jnp.float32)
    solutions = pl.pallas_call(
        functools.partial(solve, leaf_count, block_count, block_rows),
        out_shape=(kept, kept),
        in_specs=[
            pl.BlockSpec(memory_space=pltpu.SMEM),
            pl.BlockSpec(memory_space=pltpu.VMEM),
            pl.BlockSpec(memory_space=pl.ANY),
            pl.BlockSpec(memory_space=pl.ANY),
        ],
        out_specs=(
            pl.BlockSpec(memory_space=pltpu.VMEM),
            pl.BlockSpec(memory_space=pltpu.VMEM),
        ),
        scratch_shapes=[
            pltpu.VMEM(diag_inverse.shape[2:], jnp.bfloat16),
            pltpu.VMEM(update_factor.shape[2:], jnp.bfloat16),
            blocks(sizes[0]),
            upper,
            upper,
            upper,
            every,
            every,
            upper,
            pltpu.VMEM((vectors, block_rows), jnp.float32),
            blocks(8),
            pltpu.SemaphoreType.DMA((levels * (levels + 1) // 2,)),
            pltpu.SemaphoreType.DMA((phases,)),
            pltpu.SemaphoreType.DMA((phases, leaf_count)),
        ],
        compiler_params=pltpu.CompilerParams(
            collective_id=0, has_side_effects=True, vmem_limit_bytes=58 << 20
        ),
        name="solve",
    )(live_blocks, right_side, diag_inverse, update_factor)
    return pl.pallas_call(
        place,
        out_shape=(out, out),
        in_specs=[pl.BlockSpec(memory_space=pltpu.VMEM)] * 2,
        compiler_params=pltpu.CompilerParams(vmem_limit_bytes=1 << 20),
        out_specs=(pl.BlockSpec(memory_space=pl.ANY),) * 2,
        scratch_shapes=[pltpu.SemaphoreType.DMA((2,))],
        name="place",
    )(*solutions)


def solution(mesh):
    return jax.shard_map(
        functools.partial(local, mesh.shape["leaf"], mesh.shape["blk"]),
        mesh=mesh,
        in_specs=(
            P(None, "leaf", "blk", None),
            P("leaf", "blk", None, None),
            P("leaf", "blk", None, None),
            P(),
        ),
        out_specs=(P(None, "leaf", "blk", None), P(None, "leaf", "blk", None)),
        check_vma=False,
    )
```
